128 devices in a mesh: head: 4 (over y_hi, core), seq: 32 (over z, x, y_lo).
Axes of the slice: x: 4, y: 4 (y_hi: 2, y_lo: 2; y = y_hi * 2 + y_lo), z: 4, core: 2. Of those that a mesh axis runs over, the one named last changes fastest.
Arguments:
- query_rows: bfloat16 [65536, 2048], P(('head', 'seq')), may hold values from -6 to 6
- key_rows: bfloat16 [65536, 2048], P(('head', 'seq')), may hold values from -6 to 6
- value_rows: bfloat16 [65536, 2048], P(('head', 'seq')), may hold values from -6 to 6
- token_rate: bfloat16 [65536, 4], P(('head', 'seq')), may hold values from 0.099609375 to 3
- gate_fast: bfloat16 [4, 512, 512], P('head'), may hold values from -0.25 to 0.25
- lift_fast: bfloat16 [4, 512, 512], P('head'), may hold values from -0.25 to 0.25
- down_fast: bfloat16 [4, 512, 512], P('head'), may hold values from -0.25 to 0.25
- norm_gain: float32 [2048], replicated, may hold values from 0.25 to 1.75
Outputs:
- layer_out: bfloat16 [65536, 2048], P(('head', 'seq'))
The draws below stay inside these ranges and needn't reach their ends.
All inputs are finite; a program needn't handle non-finite values.
Results may differ from the reference program's by a relative error of at most 0.03.
Values may be sent and summed in bfloat16 or wider, within the bound.
No kernel may reach another device: no remote copies, remote signals or barrier semaphores. Data moves between devices by JAX's collectives and lax.ppermute only.
A program may use at most 128 MiB of HBM per device.

```python
import math
import jax
import jax.numpy as jnp
from jax import lax

HEADS = 4
DH = 512
FH = 512
WINDOW = 512
NS_STEPS = 5
D = 2048
TOKENS = 65536


def draw_query_rows(key, part):
    result = jnp.clip(jax.random.normal(jax.random.fold_in(key, 1), (TOKENS, D), jnp.float32), -6.0, 6.0)
    return result.astype(jnp.bfloat16)


def draw_key_rows(key, part):
    result = jnp.clip(jax.random.normal(jax.random.fold_in(key, 2), (TOKENS, D), jnp.float32), -6.0, 6.0)
    return result.astype(jnp.bfloat16)


def levels(key, dims, pieces, least, largest):
    gain = 1.0
    for dim, blocks in pieces:
        steps = jax.random.uniform(jax.random.fold_in(jax.random.fold_in(key, 6), dim), (blocks,), jnp.float32, least / len(pieces), largest / len(pieces))
        gain = gain * jnp.repeat(jnp.exp(steps), dims[dim] // blocks).reshape((-1,) + (1,) * (len(dims) - 1 - dim))
    return gain


def normal_values(rng, shape, spread, limit, pieces=(), kind=jnp.bfloat16):
    gain = levels(rng, shape, pieces, -0.22, 0.18) if pieces else 1.0
    array = jax.random.normal(rng, shape, jnp.float32) * spread * gain
    return jnp.minimum(jnp.maximum(array, -limit), limit).astype(kind)


def setup_inputs(seed: int = 0) -> dict:
    streams_of = jax.random.split(jax.random.key(seed), 9)
    return {
        "query_rows": draw_query_rows(jax.random.fold_in(streams_of[8], 71), 0),
        "key_rows": draw_key_rows(jax.random.fold_in(streams_of[8], 71), 0),
        "value_rows": normal_values(streams_of[2], (TOKENS, D), 1.0, 6.0, ((0, 128),)),
        "token_rate": jnp.clip(jnp.exp(math.log(3.0) - 3.4051113 * jax.random.uniform(streams_of[3], (TOKENS, HEADS), jnp.float32) ** levels(streams_of[3], (TOKENS, HEADS), ((0, 128),), -0.2, 0.2)), 0.099609375, 3.0).astype(jnp.bfloat16),
        "gate_fast": normal_values(streams_of[4], (HEADS, DH, FH), DH ** -0.5, 0.25, ((0, 4),)),
        "lift_fast": normal_values(streams_of[5], (HEADS, DH, FH), DH ** -0.5, 0.25, ((0, 4),)),
        "down_fast": normal_values(streams_of[6], (HEADS, FH, DH), FH ** -0.5, 0.25, ((0, 4),)),
        "norm_gain": jnp.clip(1.0 + 0.15 * jax.random.normal(streams_of[7], (D,), jnp.float32), 0.25, 1.75),
    }


first_coeff = 3.4445
second_coeff = -4.775
third_coeff = 2.0315
fast_rate = 0.5
norm_eps = 1e-07
rms_eps = 1e-06
neg_fill = -1e+30

def window_attention(query_rows, keys_all, values_all):
    length, width = query_rows.shape
    head_size = width // HEADS
    block_size = min(length, 512)
    block_count = length // block_size
    scale = 1.0 / math.sqrt(head_size)

    def one_block(block_index):
        first = block_index * block_size
        query_block = lax.dynamic_slice_in_dim(query_rows, first, block_size, 0).reshape(block_size, HEADS, head_size)
        key_block = lax.dynamic_slice_in_dim(keys_all, first, block_size + WINDOW, 0).reshape(block_size + WINDOW, HEADS, head_size)
        value_block = lax.dynamic_slice_in_dim(values_all, first, block_size + WINDOW, 0).reshape(block_size + WINDOW, HEADS, head_size)
        scores = jnp.einsum('qhd,khd->hqk', query_block.astype(jnp.float32), key_block.astype(jnp.float32), precision=lax.Precision.HIGHEST) * scale
        query_pos = first + jnp.arange(block_size, dtype=jnp.int32)
        key_pos = first - WINDOW + jnp.arange(block_size + WINDOW, dtype=jnp.int32)
        distance = query_pos[:, None] - key_pos[None, :]
        allowed = (distance >= 0) & (distance < WINDOW) & (key_pos[None, :] >= 0)
        scores = jnp.where(allowed[None], scores, neg_fill)
        maximum = lax.optimization_barrier(jnp.max(scores, axis=-1, keepdims=True))
        exponent = jnp.exp(scores - maximum)
        probs = (exponent / lax.optimization_barrier(jnp.sum(exponent, axis=-1, keepdims=True))).astype(jnp.bfloat16)
        mixed = jnp.einsum('hqk,khd->qhd', probs.astype(jnp.float32), value_block.astype(jnp.float32), precision=lax.Precision.HIGHEST)
        return mixed.reshape(block_size, width)
    blocks = lax.map(one_block, jnp.arange(block_count, dtype=jnp.int32))
    return blocks.reshape(length, width)

def swiglu_grads(key_part, value_part, rate_part, gate_w, lift_w, down_w):
    gate_linear = jnp.dot(key_part, gate_w, preferred_element_type=jnp.float32)
    lift_linear = jnp.dot(key_part, lift_w, preferred_element_type=jnp.float32)
    gate_sigmoid = jax.nn.sigmoid(gate_linear)
    active = gate_linear * gate_sigmoid
    hidden = (active * lift_linear).astype(jnp.bfloat16)
    upstream = (-(rate_part.astype(jnp.float32) * value_part.astype(jnp.float32))).astype(jnp.bfloat16)
    grad_down = jnp.dot(hidden.T, upstream, preferred_element_type=jnp.float32)
    back_grad = jnp.dot(upstream, down_w.T, preferred_element_type=jnp.float32)
    d_gate = (back_grad * lift_linear * gate_sigmoid * (1.0 + gate_linear * (1.0 - gate_sigmoid))).astype(jnp.bfloat16)
    d_lift = (back_grad * active).astype(jnp.bfloat16)
    grad_gate = jnp.dot(key_part.T, d_gate, preferred_element_type=jnp.float32)
    grad_lift = jnp.dot(key_part.T, d_lift, preferred_element_type=jnp.float32)
    return (grad_gate, grad_lift, grad_down)

def scale_to_unit(matrix, square_sum):
    return (matrix / (jnp.sqrt(square_sum) + norm_eps)).astype(jnp.bfloat16)

def newton_steps(current):
    for repeat in range(NS_STEPS):
        gram_matrix = jnp.dot(current, current.T, preferred_element_type=jnp.float32).astype(jnp.bfloat16)
        poly_term = (second_coeff * gram_matrix.astype(jnp.float32) + third_coeff * jnp.dot(gram_matrix, gram_matrix, preferred_element_type=jnp.float32)).astype(jnp.bfloat16)
        current = (first_coeff * current.astype(jnp.float32) + jnp.dot(poly_term, current, preferred_element_type=jnp.float32)).astype(jnp.bfloat16)
    return current

def updated(weight, start):
    return (weight.astype(jnp.float32) - fast_rate * newton_steps(start).astype(jnp.float32)).astype(jnp.bfloat16)

def swiglu_apply(query_part, gate_w, lift_w, down_w):
    gate_linear = jnp.dot(query_part, gate_w, preferred_element_type=jnp.float32)
    lift_linear = jnp.dot(query_part, lift_w, preferred_element_type=jnp.float32)
    fast_mid = (jax.nn.silu(gate_linear) * lift_linear).astype(jnp.bfloat16)
    fast_out = jnp.dot(fast_mid, down_w, preferred_element_type=jnp.float32)
    normed = fast_out * lax.rsqrt(lax.optimization_barrier(jnp.mean(fast_out * fast_out, axis=-1, keepdims=True)) + rms_eps)
    return normed.astype(jnp.bfloat16)

def reference(query_rows, key_rows, value_rows, token_rate, gate_fast, lift_fast, down_fast, norm_gain):
    width = query_rows.shape[1]
    padding = jnp.zeros((WINDOW, width), key_rows.dtype)
    attended = window_attention(query_rows, jnp.concatenate([padding, key_rows], axis=0), jnp.concatenate([padding, value_rows], axis=0))

    def per_head(head_index):
        first = head_index * DH
        key_part = lax.dynamic_slice_in_dim(key_rows, first, DH, 1)
        value_part = lax.dynamic_slice_in_dim(value_rows, first, DH, 1)
        query_part = lax.dynamic_slice_in_dim(query_rows, first, DH, 1)
        rate_part = lax.dynamic_slice_in_dim(token_rate, head_index, 1, 1)
        gate_w = gate_fast[head_index]
        lift_w = lift_fast[head_index]
        down_w = down_fast[head_index]
        grad_gate, grad_lift, grad_down = swiglu_grads(key_part, value_part, rate_part, gate_w, lift_w, down_w)
        new_gate = updated(gate_w, scale_to_unit(grad_gate, jnp.sum(grad_gate * grad_gate)))
        new_lift = updated(lift_w, scale_to_unit(grad_lift, jnp.sum(grad_lift * grad_lift)))
        new_down = updated(down_w, scale_to_unit(grad_down, jnp.sum(grad_down * grad_down)))
        return swiglu_apply(query_part, new_gate, new_lift, new_down)
    heads_out = lax.map(per_head, jnp.arange(HEADS, dtype=jnp.int32))
    merged = jnp.transpose(heads_out, (1, 0, 2)).reshape(query_rows.shape[0], width)
    return (attended + norm_gain[None, :] * merged.astype(jnp.float32)).astype(jnp.bfloat16)
```

```python
import math

import jax
import jax.numpy as jnp
from jax import lax
from jax.sharding import Mesh, PartitionSpec as P

HEADS = 4
WINDOW = 512
NS_STEPS = 5


first_coeff = 3.4445
second_coeff = -4.775
third_coeff = 2.0315
fast_rate = 0.5
norm_eps = 1e-07
rms_eps = 1e-06
neg_fill = -1e30


HEAD = ("yh", "core")
PLANE = ("z", "x")
ALL = ("yh", "core", "z", "x", "yl")


def sum_over_tokens(parts):
    rows = jnp.concatenate([part.astype(jnp.bfloat16) for part in parts], axis=0)
    peers = lax.axis_size(PLANE)
    height = rows.shape[0] // peers
    got = lax.all_to_all(rows.reshape(peers, height, -1), PLANE, 0, 0, tiled=False)
    mine = jnp.sum(got.astype(jnp.float32), axis=0).astype(jnp.bfloat16)
    other = lax.ppermute(mine, "yl", [(0, 1), (1, 0)])
    total = (mine.astype(jnp.float32) + other.astype(jnp.float32)).astype(jnp.bfloat16)
    spread = jnp.broadcast_to(total[None], (peers,) + total.shape)
    back = lax.all_to_all(spread, PLANE, 0, 0, tiled=False)
    whole = back.reshape(rows.shape).astype(jnp.float32)
    return jnp.split(whole, len(parts), axis=0)


def from_behind(array, axis, by):
    peers = lax.axis_size(axis)
    pairs = [(i, i + by) for i in range(peers) if 0 <= i + by < peers]
    return lax.ppermute(array, axis, pairs)


def window_attention(query_rows, keys_all, values_all, offset):
    length, width = query_rows.shape
    head_size = width // HEADS
    block_size = min(length, 512)
    block_count = length // block_size
    scale = 1.0 / math.sqrt(head_size)

    def one_block(block_index):
        first = block_index * block_size
        query_block = query_rows.reshape(block_size, HEADS, head_size)
        key_block = keys_all.reshape(block_size + WINDOW, HEADS, head_size)
        value_block = values_all.reshape(block_size + WINDOW, HEADS, head_size)
        scores = (
            jnp.einsum("qhd,khd->hqk", query_block, key_block, preferred_element_type=jnp.float32)
            * scale
        )
        query_pos = offset + first + jnp.arange(block_size, dtype=jnp.int32)
        key_pos = offset - WINDOW + first + jnp.arange(block_size + WINDOW, dtype=jnp.int32)
        distance = query_pos[:, None] - key_pos[None, :]
        allowed = (distance >= 0) & (distance < WINDOW) & (key_pos[None, :] >= 0)
        scores = jnp.where(allowed[None], scores, neg_fill)
        maximum = jnp.max(scores, axis=-1, keepdims=True)
        exponent = jnp.exp(scores - maximum)
        probs = (exponent / jnp.sum(exponent, axis=-1, keepdims=True)).astype(jnp.bfloat16)
        mixed = jnp.einsum("hqk,khd->qhd", probs, value_block, preferred_element_type=jnp.float32)
        return mixed.reshape(block_size, width)

    blocks = lax.map(one_block, jnp.arange(block_count, dtype=jnp.int32))
    return blocks.reshape(length, width)


def transposed_dot(left, right):
    return lax.dot_general(
        left, right, (((0,), (0,)), ((), ())), preferred_element_type=jnp.float32
    )


def swiglu_grads(key_part, value_part, rate_part, gate_w, lift_w, down_w):
    gate_linear = jnp.dot(key_part, gate_w, preferred_element_type=jnp.float32)
    lift_linear = jnp.dot(key_part, lift_w, preferred_element_type=jnp.float32)
    gate_sigmoid = jax.nn.sigmoid(gate_linear)
    active = gate_linear * gate_sigmoid
    hidden = (active * lift_linear).astype(jnp.bfloat16)
    upstream = (-(rate_part.astype(jnp.float32) * value_part.astype(jnp.float32))).astype(
        jnp.bfloat16
    )
    grad_down = transposed_dot(hidden, upstream)
    back_grad = lax.dot_general(
        upstream, down_w, (((1,), (1,)), ((), ())), preferred_element_type=jnp.float32
    )
    d_gate = (
        back_grad * lift_linear * gate_sigmoid * (1.0 + gate_linear * (1.0 - gate_sigmoid))
    ).astype(jnp.bfloat16)
    d_lift = (back_grad * active).astype(jnp.bfloat16)
    grad_gate = transposed_dot(key_part, d_gate)
    grad_lift = transposed_dot(key_part, d_lift)
    return (grad_gate, grad_lift, grad_down)


def scale_to_unit(matrix, square_sum):
    return (matrix / (jnp.sqrt(square_sum) + norm_eps)).astype(jnp.bfloat16)


def newton_steps(current):
    for repeat in range(NS_STEPS):
        gram_matrix = lax.dot_general(
            current, current, (((1,), (1,)), ((), ())), preferred_element_type=jnp.float32
        ).astype(jnp.bfloat16)
        poly_term = (
            second_coeff * gram_matrix.astype(jnp.float32)
            + third_coeff * jnp.dot(gram_matrix, gram_matrix, preferred_element_type=jnp.float32)
        ).astype(jnp.bfloat16)
        current = (
            first_coeff * current.astype(jnp.float32)
            + jnp.dot(poly_term, current, preferred_element_type=jnp.float32)
        ).astype(jnp.bfloat16)
    return current


def updated(weight, start):
    return (
        weight.astype(jnp.float32) - fast_rate * newton_steps(start).astype(jnp.float32)
    ).astype(jnp.bfloat16)


def swiglu_apply(query_part, gate_w, lift_w, down_w):
    gate_linear = jnp.dot(query_part, gate_w, preferred_element_type=jnp.float32)
    lift_linear = jnp.dot(query_part, lift_w, preferred_element_type=jnp.float32)
    fast_mid = (jax.nn.silu(gate_linear) * lift_linear).astype(jnp.bfloat16)
    fast_out = jnp.dot(fast_mid, down_w, preferred_element_type=jnp.float32)
    normed = fast_out * lax.rsqrt(jnp.mean(fast_out * fast_out, axis=-1, keepdims=True) + rms_eps)
    return normed.astype(jnp.bfloat16)


def per_device(
    query_rows, key_rows, value_rows, token_rate, gate_fast, lift_fast, down_fast, norm_gain
):
    length = query_rows.shape[0]
    offset = lax.axis_index(ALL) * length
    prior_keys, prior_values = from_behind((key_rows, value_rows), ALL, 1)
    attended = window_attention(
        query_rows,
        jnp.concatenate([prior_keys, key_rows], axis=0),
        jnp.concatenate([prior_values, value_rows], axis=0),
        offset,
    )
    query_head, key_head, value_head, rate_head = (
        lax.all_to_all(query_rows, HEAD, split_axis=1, concat_axis=0, tiled=True),
        lax.all_to_all(key_rows, HEAD, split_axis=1, concat_axis=0, tiled=True),
        lax.all_to_all(value_rows, HEAD, split_axis=1, concat_axis=0, tiled=True),
        lax.all_to_all(token_rate, HEAD, split_axis=1, concat_axis=0, tiled=True),
    )
    gate_w = gate_fast[0]
    lift_w = lift_fast[0]
    down_w = down_fast[0]
    grad_gate, grad_lift, grad_down = swiglu_grads(
        key_head, value_head, rate_head, gate_w, lift_w, down_w
    )
    total_gate, total_lift, total_down = sum_over_tokens((grad_gate, grad_lift, grad_down))
    start_gate = scale_to_unit(total_gate, jnp.sum(total_gate * total_gate))
    start_lift = scale_to_unit(total_lift, jnp.sum(total_lift * total_lift))
    start_down = scale_to_unit(total_down, jnp.sum(total_down * total_down))
    new_gate = updated(gate_w, start_gate)
    new_lift = updated(lift_w, start_lift)
    new_down = updated(down_w, start_down)
    normed = swiglu_apply(query_head, new_gate, new_lift, new_down)
    returned = lax.all_to_all(normed, HEAD, split_axis=0, concat_axis=1, tiled=True)
    return (attended + norm_gain[None, :] * returned.astype(jnp.float32)).astype(jnp.bfloat16)


def solution(mesh):
    mesh = Mesh(mesh.devices.reshape(2, 2, 4, 4, 2), ALL)
    in_specs = (
        P(ALL, None),
        P(ALL, None),
        P(ALL, None),
        P(ALL, None),
        P(HEAD, None, None),
        P(HEAD, None, None),
        P(HEAD, None, None),
        P(),
    )
    out_specs = P(ALL, None)
    return jax.shard_map(
        per_device, mesh=mesh, in_specs=in_specs, out_specs=out_specs, check_vma=False
    )
```
